32 devices in a mesh: sample: 2 (over x), space: 16 (over z, y, core).
Axes of the slice: x: 2, y: 2, z: 4, core: 2. Of those that a mesh axis runs over, the one named last changes fastest.
Arguments:
- volume: bfloat16 [2, 128, 16, 1024], P('sample', 'space'), may hold values from -6 to 6
- cotangent: bfloat16 [2, 16, 2, 4, 256], P('sample', 'space'), may hold values from -0.375 to 0.375
- weight_first: bfloat16 [3, 3, 3, 32, 64], replicated, may hold values from -0.21875 to 0.21875
- weight_mid: bfloat16 [3, 3, 3, 64, 128], replicated, may hold values from -0.15625 to 0.15625
- weight_last: bfloat16 [3, 3, 3, 128, 256], P(None, None, None, None, 'sample'), may hold values from -0.109375 to 0.109375
Outputs:
- out_act: bfloat16 [2, 16, 2, 4, 256], P('sample', 'space')
- grad_first: float32 [3, 3, 3, 32, 64], replicated
- grad_mid: float32 [3, 3, 3, 64, 128], replicated
- grad_last: float32 [3, 3, 3, 128, 256], P(None, None, None, None, 'sample')
The draws below stay inside these ranges and needn't reach their ends.
All inputs are finite; a program needn't handle non-finite values.
Results may differ from the reference program's by a relative error of at most 0.015.
The reference program's roundings to bfloat16 on the way (of `act_first`, `act_mid`, `dact_mid`, `dpre_mid` and `dpre_first`) count: a program that leaves them out, or rounds other values in their place, can miss the bound.
Values may be sent and summed in bfloat16 or wider, within the bound.
A program may use at most 128 MiB of HBM per device.

```python
import jax
import jax.numpy as jnp
from jax import lax

C0 = 32
C1 = 64
C2 = 128
C3 = 256
Y0 = 16
Z0 = 32
SAMPLES = 2
X0 = 128
X3 = 16
Y3 = 2
Z3 = 4


def level_of(rng, dims, cuts, smallest, high):
    factor_of, own = 1.0, jax.random.fold_in(rng, 6)
    for position, shards_of in cuts:
        steps = jnp.exp(jax.random.uniform(jax.random.fold_in(own, position), (shards_of,), jnp.float32, smallest / len(cuts), high / len(cuts)))
        factor_of = factor_of * jnp.repeat(steps, dims[position] // shards_of).reshape([-1 if axis == position else 1 for axis in range(len(dims))])
    return factor_of


def scatter_about(key, shape, spread, most, cuts=(), dtype=jnp.bfloat16):
    loudness = level_of(key, shape, cuts, -0.22, 0.18) if cuts else 1.0
    result = jax.random.normal(key, shape, jnp.float32) * spread * loudness
    return jnp.minimum(jnp.maximum(result, -most), most).astype(dtype)


def setup_inputs(seed: int = 0) -> dict:
    streams_of = jax.random.split(jax.random.key(seed), 6)
    volume = scatter_about(streams_of[0], (SAMPLES, X0, Y0, Z0 * C0), 1.0, 6.0, ((0, 2), (1, 16)))
    cotangent = scatter_about(streams_of[1], (SAMPLES, X3, Y3, Z3, C3), (1.0 / (SAMPLES * X3 * Y3 * Z3) ** 0.5), 0.375, ((0, 2), (1, 16)))
    weight_first = scatter_about(streams_of[2], (3, 3, 3, C0, C1), (27 * C0) ** -0.5, 0.21875)
    weight_mid = scatter_about(streams_of[3], (3, 3, 3, C1, C2), (27 * C1) ** -0.5, 0.15625)
    weight_last = scatter_about(streams_of[4], (3, 3, 3, C2, C3), (27 * C2) ** -0.5, 0.109375, ((4, 2),))
    return {"volume": volume, "cotangent": cotangent, "weight_first": weight_first, "weight_mid": weight_mid, "weight_last": weight_last}


LEAK = 0.3

def leak_relu(value):
    return jnp.where(value > 0, value, LEAK * value)

def leak_slope(value):
    return jnp.where(value > 0, jnp.float32(1.0), jnp.float32(LEAK))

def pad_front(field):
    return jnp.pad(field, ((1, 0), (1, 0), (1, 0), (0, 0)))

def tap_slice(padded, off_x, off_y, off_z, out_x, out_y, out_z):
    chans = padded.shape[3]
    return lax.slice(padded, (off_x, off_y, off_z, 0), (off_x + 2 * out_x - 1, off_y + 2 * out_y - 1, off_z + 2 * out_z - 1, chans), (2, 2, 2, 1))

def conv_down(padded, weight):
    out_x = (padded.shape[0] - 1) // 2
    out_y = (padded.shape[1] - 1) // 2
    out_z = (padded.shape[2] - 1) // 2
    chans_in = weight.shape[3]
    chans_out = weight.shape[4]
    total = jnp.zeros((out_x * out_y * out_z, chans_out), jnp.float32)
    for off_x in range(3):
        for off_y in range(3):
            for off_z in range(3):
                piece = tap_slice(padded, off_x, off_y, off_z, out_x, out_y, out_z).reshape(-1, chans_in)
                total = total + jnp.dot(piece, weight[off_x, off_y, off_z], preferred_element_type=jnp.float32)
    return total.reshape(out_x, out_y, out_z, chans_out)

def weight_grad(padded, grad):
    out_x, out_y, out_z, chans_out = grad.shape
    chans_in = padded.shape[3]
    flat = grad.reshape(-1, chans_out)
    blocks = []
    for off_x in range(3):
        for off_y in range(3):
            for off_z in range(3):
                piece = tap_slice(padded, off_x, off_y, off_z, out_x, out_y, out_z).reshape(-1, chans_in)
                blocks.append(lax.dot_general(piece, flat, (((0,), (0,)), ((), ())), preferred_element_type=jnp.float32))
    return jnp.stack(blocks).reshape(3, 3, 3, chans_in, chans_out)

def data_grad(grad, weight):
    out_x, out_y, out_z, chans_out = grad.shape
    chans_in = weight.shape[3]
    flat = grad.reshape(-1, chans_out)
    total = jnp.zeros((2 * out_x + 1, 2 * out_y + 1, 2 * out_z + 1, chans_in), jnp.float32)
    for off_x in range(3):
        for off_y in range(3):
            for off_z in range(3):
                part = lax.dot_general(flat, weight[off_x, off_y, off_z], (((1,), (1,)), ((), ())), preferred_element_type=jnp.float32).reshape(out_x, out_y, out_z, chans_in)
                total = total.at[off_x:off_x + 2 * out_x - 1:2, off_y:off_y + 2 * out_y - 1:2, off_z:off_z + 2 * out_z - 1:2, :].add(part)
    return total

def one_sample(pair, weight_first, weight_mid, weight_last):
    volume, cotangent = pair
    chans = weight_first.shape[3]
    first_in = volume.reshape(volume.shape[0], volume.shape[1], volume.shape[2] // chans, chans)
    padded_first = pad_front(first_in)
    pre_first = conv_down(padded_first, weight_first)
    act_first = leak_relu(pre_first).astype(jnp.bfloat16)
    padded_mid = pad_front(act_first)
    pre_mid = conv_down(padded_mid, weight_mid)
    act_mid = leak_relu(pre_mid).astype(jnp.bfloat16)
    padded_last = pad_front(act_mid)
    out_act = conv_down(padded_last, weight_last).astype(jnp.bfloat16)
    grad_last = weight_grad(padded_last, cotangent)
    dact_mid = data_grad(cotangent, weight_last)[1:, 1:, 1:].astype(jnp.bfloat16)
    dpre_mid = (dact_mid.astype(jnp.float32) * leak_slope(pre_mid)).astype(jnp.bfloat16)
    grad_mid = weight_grad(padded_mid, dpre_mid)
    dact_first = data_grad(dpre_mid, weight_mid)[1:, 1:, 1:]
    dpre_first = (dact_first * leak_slope(pre_first)).astype(jnp.bfloat16)
    grad_first = weight_grad(padded_first, dpre_first)
    return (out_act, grad_first, grad_mid, grad_last)

def reference(volume, cotangent, weight_first, weight_mid, weight_last):
    results = lax.map(lambda pair: one_sample(pair, weight_first, weight_mid, weight_last), (volume, cotangent))
    return (results[0], lax.optimization_barrier(jnp.sum(results[1], axis=0)), lax.optimization_barrier(jnp.sum(results[2], axis=0)), lax.optimization_barrier(jnp.sum(results[3], axis=0)))
```

```python
import functools

import jax
import jax.numpy as jnp
from jax import lax
from jax.experimental import pallas as pl
from jax.experimental.pallas import tpu as pltpu
from jax.sharding import PartitionSpec as P

LEAK = 0.3


def leak_relu(value):
    return jnp.where(value > 0, value, LEAK * value)


def leak_slope(value):
    return jnp.where(value > 0, jnp.float32(1.0), jnp.float32(LEAK))


def shift_up(field):
    rows = field.shape[2]
    rolled = pltpu.roll(field.reshape(-1, rows, 128), 1, 1)
    keep = lax.broadcasted_iota(jnp.int32, rolled.shape, 1) > 0
    return jnp.where(keep, rolled, 0.0).reshape(field.shape)


def shift_down(field):
    rows = field.shape[2]
    rolled = pltpu.roll(field.reshape(-1, rows, 128), rows - 1, 1)
    keep = lax.broadcasted_iota(jnp.int32, rolled.shape, 1) < rows - 1
    return jnp.where(keep, rolled, 0.0).reshape(field.shape)


def tap_rows(field, rim):
    size_x, size_y, groups, lanes = field.shape
    split = field.reshape(size_x // 2, 2, size_y, groups, lanes)
    odd_x = jnp.concatenate([rim[None], split[:, 1]], axis=0)
    planes = (odd_x[:-1], split[:, 0], odd_x[1:])
    taps = []
    for plane in planes:
        count = plane.shape[0]
        parts = plane.reshape(count, size_y // 2, 2, groups, lanes)
        zero = jnp.zeros((count, 1, groups, lanes), field.dtype)
        odd_y = jnp.concatenate([zero, parts[:, :, 1]], axis=1)
        for piece in (odd_y[:, :-1], parts[:, :, 0], odd_y[:, 1:]):
            wide = jnp.concatenate([shift_up(piece), piece], axis=3)
            taps.append(wide.reshape(-1, 2 * lanes).astype(jnp.bfloat16))
    return taps


def conv_taps(taps, wide):
    total = None
    for tap, rows in enumerate(taps):
        part = jnp.dot(rows, wide[tap], preferred_element_type=jnp.float32)
        total = part if total is None else total + part
    return total


def spread_back(grad, wide, out_x, out_y, groups):
    planes = []
    for tap_x in range(3):
        pieces = []
        for tap_y in range(3):
            part = lax.dot_general(
                grad, wide[3 * tap_x + tap_y], (((1,), (1,)), ((), ())), preferred_element_type=jnp.float32
            )
            part = part.reshape(out_x, out_y, groups, 256)
            pieces.append(shift_down(part[..., :128]) + part[..., 128:])
        zero = jnp.zeros((out_x, 1, groups, 128), jnp.float32)
        odd_y = pieces[2] + jnp.concatenate([pieces[0][:, 1:], zero], axis=1)
        whole = jnp.concatenate([pieces[1][:, :, None], odd_y[:, :, None]], axis=2)
        planes.append(whole.reshape(out_x, 2 * out_y, groups, 128))
    zero = jnp.zeros((1,) + planes[0].shape[1:], jnp.float32)
    odd_x = planes[2] + jnp.concatenate([planes[0][1:], zero], axis=0)
    field = jnp.concatenate([planes[1][:, None], odd_x[:, None]], axis=1)
    return planes[0][0], field.reshape(2 * out_x, 2 * out_y, groups, 128)


def contract_rows(rows, grad):
    return lax.dot_general(rows, grad, (((0,), (0,)), ((), ())), preferred_element_type=jnp.float32)


MESH = pl.DeviceIdType.MESH
VM = pl.BlockSpec(memory_space=pltpu.VMEM)
BLOCK = 80


def roll_rows(tile, by):
    flat = tile.reshape(-1, 8, 128)
    return pltpu.roll(flat, by, 1).reshape(tile.shape)


def row_of(tile):
    return lax.broadcasted_iota(jnp.int32, tile.shape, tile.ndim - 2)


def last_taps(acts, before):
    count = acts.shape[0]
    planes = []
    for field in (acts, before):
        even = field[:, :32].reshape(count, 2, 2, 8, 128)
        odd = field[:, 32:64].reshape(count, 2, 2, 8, 128)
        moved = roll_rows(odd, 1)
        moved = jnp.where(lax.rem(row_of(moved), 4) > 0, moved, 0.0)
        planes.append((moved, even, odd))
    taps = []
    for tap_x in range(3):
        for tap_y in range(3):
            for tap_z in range(3):
                tiles = planes[1 if tap_x == 0 else 0][tap_z][:, 0 if tap_x == 1 else 1]
                low, high = tiles[:, 0], tiles[:, 1]
                upper = row_of(low) < 4
                if tap_y == 0:
                    rows = jnp.where(upper, 0.0, low)
                elif tap_y == 1:
                    rows = jnp.where(upper, low, roll_rows(high, 4))
                else:
                    rows = jnp.where(upper, roll_rows(low, 4), high)
                taps.append(rows.reshape(count * 8, 128).astype(jnp.bfloat16))
    return taps


def last_back(cots, weight_last, samples):
    flat = cots.reshape(samples * 16, -1)

    def part(tap_x, tap_y, tap_z):
        value = lax.dot_general(
            flat,
            weight_last[9 * tap_x + 3 * tap_y + tap_z],
            (((1,), (1,)), ((), ())),
            preferred_element_type=jnp.float32,
        )
        return value.reshape(samples, 2, 8, 128)

    tiles = ([], [])
    for plane in range(2):
        rows = [[None] * 3 for _ in range(3)]
        for tap_y in range(3):
            for tap_z in range(3):
                if plane == 0:
                    rows[tap_y][tap_z] = part(1, tap_y, tap_z)[:, 0]
                else:
                    rows[tap_y][tap_z] = part(2, tap_y, tap_z)[:, 0] + part(0, tap_y, tap_z)[:, 1]
        for parity in range(2):
            picked = []
            for tap_y in range(3):
                if parity == 0:
                    picked.append(rows[tap_y][1])
                else:
                    moved = roll_rows(rows[tap_y][0], 7)
                    moved = jnp.where(lax.rem(row_of(moved), 4) < 3, moved, 0.0)
                    picked.append(rows[tap_y][2] + moved)
            upper = row_of(picked[0]) < 4
            tiles[parity].append(jnp.where(upper, picked[1], roll_rows(picked[2], 4) + picked[0]))
            tiles[parity].append(jnp.where(upper, roll_rows(picked[1], 4), picked[2]))
    return jnp.concatenate(tiles[0] + tiles[1], axis=1)


def whole_kernel(
    samples, spaces, dims, rows_each,
    volume, cotangent, weight_first, weight_mid, weight_last,
    out_act, result, grad_last,
    cells, rim_cells, half_sem, last_sem, rim, act_send, act_rim, back_send, back_rim,
    cot_in, dact_send, dact_in, mid_rows, block, blocks,
    data, half_in, mine, parts, done, out_send, out_in,
    ring, cot_sem, swap, send, recv, pair_sem, gather_send, gather_recv, out_sem,
):
    size_x, size_y, groups = dims
    sample = lax.axis_index("sample")
    space = lax.axis_index("space")
    core = lax.rem(space, 2)
    pairs = spaces // 2
    chips = samples * pairs
    chip = sample * pairs + space // 2
    filters = weight_last.shape[2]

    def at(by_sample, by_space):
        return {
            "sample": lax.rem(sample + by_sample, samples),
            "space": lax.rem(space + by_space + spaces, spaces),
        }

    def peer(to):
        return {"sample": to // pairs, "space": lax.rem(to, pairs) * 2 + core}

    partner = {"sample": sample, "space": space + 1 - 2 * core}
    barrier = pltpu.get_barrier_semaphore()
    near = [partner] + [at(by, step) for by in range(samples) for step in (1, -1)]
    for device in near:
        pl.semaphore_signal(barrier, inc=1, device_id=device, device_id_type=MESH)

    def tell(step, carry):
        pl.semaphore_signal(
            barrier, inc=1, device_id=peer(lax.rem(chip + step, chips)), device_id_type=MESH
        )
        return carry

    lax.fori_loop(1, chips, tell, 0)
    pl.semaphore_wait(barrier, chips - 1 + len(near))

    def link(source, target, sems, slot, device):
        return pltpu.make_async_remote_copy(
            src_ref=source,
            dst_ref=target,
            send_sem=sems.at[2 * slot],
            recv_sem=sems.at[2 * slot + 1],
            device_id=device,
            device_id_type=MESH,
        )

    cot_copies = []
    for by in range(samples):
        for ahead in range(2):
            if by or ahead:
                slot = 2 * by + ahead
                cot_copies.append(
                    link(cotangent, cot_in.at[ahead, by], cot_sem, slot, at(by, -ahead))
                )
                cot_copies[-1].start()
    first = link(volume.at[pl.ds((size_x - 1) * size_y, size_y)], rim, ring, 0, at(0, 1))
    first.start()

    def pick(value):
        kept = value[..., :filters]
        for shard in range(1, samples):
            kept = jnp.where(sample == shard, value[..., shard * filters : (shard + 1) * filters], kept)
        return kept

    def cells_of(value):
        wide = value.astype(jnp.float32)
        return jnp.concatenate([wide[0], wide[1]], axis=0)

    own_cot = cells_of(cotangent[...])
    block[64:80] = jnp.concatenate([own_cot[:, :128], own_cot[:, 128:]], axis=0).astype(jnp.bfloat16)
    for group in range(groups):
        lanes = volume[:, 128 * group : 128 * group + 128].astype(jnp.float32)
        cells[pl.ds(group, size_x * size_y, stride=groups), :] = lanes
    flat_first = weight_first[...].astype(jnp.float32)
    wide_first, wide_mid = [], []
    for tap in range(9):
        piece = flat_first[96 * tap : 96 * tap + 96]
        gap = jnp.zeros((96, 64), jnp.float32)
        left = jnp.concatenate([gap, piece, gap[:64]], axis=0)
        right = jnp.concatenate([gap, gap[:64], piece], axis=0)
        wide_first.append(jnp.concatenate([left, right], axis=1).astype(jnp.bfloat16))
        piece = weight_mid[192 * tap : 192 * tap + 192]
        wide_mid.append(jnp.concatenate([jnp.zeros((64, 128), jnp.bfloat16), piece], axis=0))

    for copy in cot_copies:
        copy.wait()
    cots = []
    for by in range(samples):
        own = own_cot if by == 0 else cells_of(cot_in[0, by])
        nxt = jnp.where(space < spaces - 1, cells_of(cot_in[1, by]), 0.0)
        cots.append(pick(own))
        cots.append(pick(nxt))
    cots = jnp.concatenate(cots, axis=0).astype(jnp.bfloat16)
    dact_send[...] = last_back(cots, weight_last, samples).astype(jnp.bfloat16)
    swaps = []
    for by in range(1, samples):
        swaps.append(link(dact_send.at[by], dact_in.at[by], swap, by, at(samples - by, 0)))
        swaps[-1].start()

    first.wait()
    field = cells[...].reshape(size_x, size_y, groups, 128)
    for group in range(groups):
        lanes = rim[:, 128 * group : 128 * group + 128].astype(jnp.float32)
        rim_cells[pl.ds(group, size_y, stride=groups), :] = jnp.where(space > 0, lanes, 0.0)
    edge = rim_cells[...].reshape(size_y, groups, 128)
    taps_first = tap_rows(field, edge)
    pre_first = conv_taps(taps_first, wide_first)
    act_first = leak_relu(pre_first).astype(jnp.bfloat16)
    half = (size_x // 2, size_y // 2)
    side = half[1] * groups
    act_send[...] = act_first[-side:]
    second = link(act_send, act_rim, ring, 1, at(0, 1))
    second.start()
    second.wait()
    edge = jnp.where(space > 0, act_rim[...].astype(jnp.float32), 0.0).reshape(half[1], groups, 128)
    taps_mid = tap_rows(act_first.astype(jnp.float32).reshape(half + (groups, 128)), edge)
    pre_mid = conv_taps(taps_mid, wide_mid)
    mid_rows[...] = leak_relu(pre_mid).astype(jnp.bfloat16).astype(jnp.float32)
    block[:32] = mid_rows[pl.ds(0, 32, stride=2), :].astype(jnp.bfloat16)
    block[32:64] = mid_rows[pl.ds(1, 32, stride=2), :].astype(jnp.bfloat16)

    def gather(step, slot):
        return pltpu.make_async_remote_copy(
            src_ref=block,
            dst_ref=blocks.at[slot, core],
            send_sem=gather_send.at[step],
            recv_sem=gather_recv.at[step],
            device_id=peer(lax.rem(chip + step, chips)),
            device_id_type=MESH,
        )

    def start_gather(step, carry):
        gather(step, chip).start()
        return carry

    def wait_gather(step, carry):
        gather(step, lax.rem(chip + chips - step, chips)).wait()
        return carry

    for copy in swaps:
        copy.wait()
    total = dact_send[0].astype(jnp.float32)
    for by in range(1, samples):
        total = total + dact_in[by].astype(jnp.float32)
    total = total.astype(jnp.bfloat16).astype(jnp.float32)
    mid_rows[pl.ds(0, 32, stride=2), :] = total[:32]
    mid_rows[pl.ds(1, 32, stride=2), :] = total[32:]
    dpre_mid = (mid_rows[...] * leak_slope(pre_mid)).astype(jnp.bfloat16)
    back, dact_first = spread_back(dpre_mid, wide_mid, half[0] // 2, half[1] // 2, groups)
    back_send[...] = back.reshape(side, 128).astype(jnp.bfloat16)
    third = link(back_send, back_rim, ring, 2, at(0, -1))
    third.start()
    lax.fori_loop(1, chips, start_gather, 0)
    kept = pltpu.make_async_copy(block, blocks.at[chip, core], pair_sem.at[6])
    kept.start()
    row = 0
    for taps in taps_mid:
        data[row : row + 192] = contract_rows(taps, dpre_mid)[64:].astype(jnp.bfloat16)
        row += 192
    third.wait()
    edge = jnp.where(space < spaces - 1, back_rim[...].astype(jnp.float32), 0.0)
    flat = dact_first.reshape(-1, 128)
    flat = jnp.concatenate([flat[:-side], flat[-side:] + edge], axis=0)
    dpre_first = (flat * leak_slope(pre_first)).astype(jnp.bfloat16)
    for taps in taps_first:
        part = contract_rows(taps, dpre_first)
        part = part[96:192, :64] + part[160:256, 64:]
        part = jnp.concatenate([part[:48], part[48:]], axis=1)
        data[row : row + 48] = part.astype(jnp.bfloat16)
        row += 48
    data[row:] = jnp.zeros((data.shape[0] - row, 128), jnp.bfloat16)

    span = chips * rows_each

    def rows_at(side_of, slot):
        return pl.ds(pl.multiple_of(side_of * span + slot * rows_each, 16), rows_each)

    def pair_link(source, target, sems, step):
        return pltpu.make_async_remote_copy(
            src_ref=source,
            dst_ref=target,
            send_sem=sems.at[step],
            recv_sem=sems.at[chips + step],
            device_id=partner,
            device_id_type=MESH,
        )

    def halves(step):
        slot = lax.rem(chip + step, chips)
        return pair_link(data.at[rows_at(1 - core, slot)], half_in.at[step], half_sem, step)

    def start_halves(step, carry):
        halves(step).start()
        return carry

    lax.fori_loop(1, chips, start_halves, 0)
    halves(0).start()

    def own_half(step):
        halves(step).wait()
        rows = data[rows_at(core, lax.rem(chip + step, chips))].astype(jnp.float32)
        return rows + half_in[step].astype(jnp.float32)

    def scatter(step):
        to = lax.rem(chip + step, chips)
        return pltpu.make_async_remote_copy(
            src_ref=mine.at[step],
            dst_ref=parts.at[step],
            send_sem=send.at[step],
            recv_sem=recv.at[step],
            device_id=peer(to),
            device_id_type=MESH,
        )

    def start_scatter(step, carry):
        mine[step] = own_half(step).astype(jnp.bfloat16)
        scatter(step).start()
        return carry

    lax.fori_loop(1, chips, start_scatter, 0)
    kept.wait()
    lax.fori_loop(1, chips, wait_gather, 0)
    share = link(blocks.at[:, core], blocks.at[:, core], pair_sem, 1, partner)
    share.start()
    share.wait_send()
    link(blocks.at[:, 1 - core], blocks.at[:, 1 - core], pair_sem, 1, partner).wait_recv()


    chunk = min(spaces, 16)
    chunks = spaces // chunk
    grad_last[...] = jnp.zeros(grad_last.shape, jnp.float32)

    def contract_last(step, carry):
        start = (step // chunks) * pairs + lax.rem(step, chunks) * (chunk // 2)
        acts = blocks[pl.ds(start, chunk // 2)].astype(jnp.float32).reshape(chunk, BLOCK, 128)
        ahead = blocks[lax.max(start - 1, 0), 1].astype(jnp.float32)
        ahead = jnp.where(lax.rem(step, chunks) > 0, ahead, 0.0)
        before = jnp.concatenate([ahead[None], acts[:-1]], axis=0)
        grads_out = jnp.concatenate([acts[:, 64:72], acts[:, 72:80]], axis=2).reshape(chunk * 8, 256)
        grads_out = pick(grads_out).astype(jnp.bfloat16)
        for tap, rows in enumerate(last_taps(acts, before)):
            grad_last[tap] += contract_rows(rows, grads_out)
        return carry

    steps = samples * chunks
    lax.fori_loop(0, steps // 2, contract_last, 0)

    def collect(step, total):
        scatter(step).wait()
        return total + parts[step].astype(jnp.float32)

    done[...] = lax.fori_loop(1, chips, collect, own_half(0)).astype(jnp.bfloat16)

    def spread(step, slot):
        return pltpu.make_async_remote_copy(
            src_ref=done,
            dst_ref=result.at[rows_at(core, slot)],
            send_sem=send.at[chips + step],
            recv_sem=recv.at[chips + step],
            device_id=peer(lax.rem(chip + step, chips)),
            device_id_type=MESH,
        )

    def start_spread(step, carry):
        spread(step, chip).start()
        return carry

    def forward(source, side_of, step):
        slot = lax.rem(chip + chips - step, chips)
        return pair_link(source, result.at[rows_at(side_of, slot)], last_sem, step)

    def wait_spread(step, carry):
        slot = lax.rem(chip + chips - step, chips)
        spread(step, slot).wait()
        forward(result.at[rows_at(core, slot)], core, step).start()
        return carry

    def wait_forward(step, carry):
        slot = lax.rem(chip + chips - step, chips)
        forward(result.at[rows_at(core, slot)], core, step).wait_send()
        forward(result.at[rows_at(1 - core, slot)], 1 - core, step).wait_recv()
        return carry

    lax.fori_loop(1, chips, start_spread, 0)
    forward(done, core, 0).start()
    own = pltpu.make_async_copy(done, result.at[rows_at(core, chip)], pair_sem.at[7])
    own.start()

    here, behind = [], []
    earlier = lax.rem(space + spaces - 1, spaces)
    for by in range(samples):
        base = lax.rem(sample + by, samples) * pairs
        here.append(blocks[base + space // 2, core].astype(jnp.float32))
        behind.append(blocks[base + earlier // 2, lax.rem(earlier, 2)].astype(jnp.float32))
    behind = jnp.where(space > 0, jnp.stack(behind), 0.0)
    taps_last = last_taps(jnp.stack(here), behind)
    outputs = conv_taps(taps_last, weight_last).reshape(samples, 8, filters)
    out_send[...] = outputs
    out_copies = []
    for by in range(1, samples):
        out_copies.append(link(out_send.at[by], out_in.at[by], out_sem, by, at(by, 0)))
        out_copies[-1].start()

    lax.fori_loop(steps // 2, steps, contract_last, 0)
    for copy in out_copies:
        copy.wait()
    shards = []
    for shard in range(samples):
        value = out_send[0]
        for by in range(1, samples):
            value = jnp.where(lax.rem(sample + samples - by, samples) == shard, out_in[by], value)
        shards.append(value)
    shards = jnp.concatenate(shards, axis=1).astype(jnp.bfloat16)
    out_act[0] = shards[:4]
    out_act[1] = shards[4:]
    own.wait()
    lax.fori_loop(1, chips, wait_spread, 0)
    forward(done, core, 0).wait_send()
    forward(done, 1 - core, 0).wait_recv()
    lax.fori_loop(1, chips, wait_forward, 0)


def write_kernel(act, summed, last, out_act, grad_first, grad_mid, grad_last, first, mid, sems):
    copies = [pltpu.make_async_copy(last, grad_last, sems.at[0])]
    copies[-1].start()
    copies.append(pltpu.make_async_copy(act, out_act, sems.at[1]))
    copies[-1].start()
    rows = mid.shape[0]
    mid[...] = summed[:rows].astype(jnp.float32)
    copies.append(pltpu.make_async_copy(mid, grad_mid, sems.at[2]))
    copies[-1].start()
    for tap in range(9):
        tail = summed[rows + 48 * tap : rows + 48 * tap + 48].astype(jnp.float32)
        first[96 * tap : 96 * tap + 48] = tail[:, :64]
        first[96 * tap + 48 : 96 * tap + 96] = tail[:, 64:]
    copies.append(pltpu.make_async_copy(first, grad_first, sems.at[3]))
    copies[-1].start()
    for copy in copies:
        copy.wait()


def per_device(volume, cotangent, weight_first, weight_mid, weight_last):
    samples = lax.axis_size("sample")
    spaces = lax.axis_size("space")
    chips = samples * spaces // 2
    size_x, size_y, deep = volume.shape[1:]
    groups = deep // 128
    filters = weight_last.shape[4]
    edge = size_y * groups // 2
    count = 27 * 64 + 27 * 16
    rows_each = -(-count // (32 * chips)) * 16
    half = (chips * rows_each, 128)
    b16 = jnp.bfloat16
    dma = pltpu.SemaphoreType.DMA
    out_act, summed, grad_last = pl.pallas_call(
        functools.partial(whole_kernel, samples, spaces, (size_x, size_y, groups), rows_each),
        out_shape=[
            pltpu.VMEM(cotangent.shape[2:], b16),
            pltpu.VMEM((2 * half[0], 128), b16),
            pltpu.VMEM((27, 128, filters), jnp.float32),
        ],
        in_specs=[VM] * 5,
        out_specs=[VM] * 3,
        scratch_shapes=[
            pltpu.VMEM((size_x * size_y * groups, 128), jnp.float32),
            pltpu.VMEM((size_y * groups, 128), jnp.float32),
            dma((2 * chips,)),
            dma((2 * chips,)),
            pltpu.VMEM((size_y, deep), b16),
            pltpu.VMEM((edge, 128), b16),
            pltpu.VMEM((edge, 128), b16),
            pltpu.VMEM((edge, 128), b16),
            pltpu.VMEM((edge, 128), b16),
            pltpu.VMEM((2, samples) + cotangent.shape[2:], b16),
            pltpu.VMEM((samples, 64, 128), b16),
            pltpu.VMEM((samples, 64, 128), b16),
            pltpu.VMEM((64, 128), jnp.float32),
            pltpu.VMEM((BLOCK, 128), b16),
            pltpu.VMEM((chips, 2, BLOCK, 128), b16),
            pltpu.VMEM((2 * half[0], 128), b16),
            pltpu.VMEM((chips, rows_each, 128), b16),
            pltpu.VMEM((chips, rows_each, 128), b16),
            pltpu.VMEM((chips, rows_each, 128), b16),
            pltpu.VMEM((rows_each, 128), b16),
            pltpu.VMEM((samples, 8, filters), jnp.float32),
            pltpu.VMEM((samples, 8, filters), jnp.float32),
            dma((6,)),
            dma((4 * samples,)),
            dma((2 * samples,)),
            dma((2 * chips,)),
            dma((2 * chips,)),
            dma((8,)),
            dma((chips,)),
            dma((chips,)),
            dma((2 * samples,)),
        ],
        compiler_params=pltpu.CompilerParams(collective_id=0, has_side_effects=True, vmem_limit_bytes=40 << 20),
        name="whole",
    )(
        volume.reshape(-1, deep),
        cotangent.reshape(cotangent.shape[2:]),
        weight_first.reshape(27 * 32, 64),
        weight_mid.reshape(27 * 64, 128),
        weight_last.reshape(27, 128, filters),
    )
    any_spec = pl.BlockSpec(memory_space=pl.ANY)
    out_act, grad_first, grad_mid, grad_last = pl.pallas_call(
        write_kernel,
        out_shape=[
            jax.ShapeDtypeStruct(cotangent.shape[2:], b16),
            jax.ShapeDtypeStruct((27 * 32, 64), jnp.float32),
            jax.ShapeDtypeStruct((27 * 64, 128), jnp.float32),
            jax.ShapeDtypeStruct((27, 128, filters), jnp.float32),
        ],
        in_specs=[VM] * 3,
        out_specs=[any_spec] * 4,
        scratch_shapes=[
            pltpu.VMEM((27 * 32, 64), jnp.float32),
            pltpu.VMEM((27 * 64, 128), jnp.float32),
            dma((4,)),
        ],
        compiler_params=pltpu.CompilerParams(vmem_limit_bytes=16 << 20),
        name="write",
    )(*[pltpu.with_memory_space_constraint(value, pltpu.VMEM) for value in (out_act, summed, grad_last)])
    return (
        out_act.reshape(cotangent.shape),
        grad_first.reshape(weight_first.shape),
        grad_mid.reshape(weight_mid.shape),
        grad_last.reshape(weight_last.shape),
    )


def solution(mesh):
    in_specs = (
        P("sample", "space", None, None),
        P("sample", "space", None, None, None),
        P(),
        P(),
        P(None, None, None, None, "sample"),
    )
    out_specs = (
        P("sample", "space", None, None, None),
        P(),
        P(),
        P(None, None, None, None, "sample"),
    )
    return jax.shard_map(
        per_device, mesh=mesh, in_specs=in_specs, out_specs=out_specs, check_vma=False
    )
```
